32 devices in a mesh: ctx: 4 (over z), head: 8 (over y, x, core).
Axes of the slice: x: 2, y: 2, z: 4, core: 2. Of those that a mesh axis runs over, the one named last changes fastest.
Arguments:
- query_rows: bfloat16 [1024, 16384], P('ctx', 'head'), may hold values from -5 to 5
- key_rows: bfloat16 [1024, 1024], P('ctx'), may hold values from -5 to 5
- value_rows: bfloat16 [1024, 1024], P('ctx'), may hold values from -6 to 6
- out_grad: bfloat16 [1024, 16384], P('ctx', 'head'), may hold values from -16 to 16
- span_order: int32 [8], replicated, may hold values from 0 to 7, as said below
Outputs:
- attn_out: bfloat16 [1024, 16384], P('ctx', 'head')
- query_grad: bfloat16 [1024, 16384], P('ctx', 'head')
- key_grad: bfloat16 [1024, 1024], P(('ctx', 'head'))
- value_grad: bfloat16 [1024, 1024], P(('ctx', 'head'))
The draws below stay inside these ranges and needn't reach their ends.
Inputs may be any that keep to these rules, and one draw needn't show every extreme that they name: `span_order`: each of 0 to 7 appears once, and entries 2d and 2d + 1 add up to 7.
All inputs are finite; a program needn't handle non-finite values.
Results may differ from the reference program's by a relative error of at most 0.025.
Values may be sent and summed in bfloat16 or wider, within the bound.
No kernel may reach another device: no remote copies, remote signals or barrier semaphores. Data moves between devices by JAX's collectives and lax.ppermute only.
A program may use at most 64 MiB of HBM per device.

```python
import math
import jax
import jax.numpy as jnp
from jax import lax

QUERY_HEADS = 128
KV_HEADS = 8
HEAD_DIM = 128
SPAN = 128
SPANS = 8
SEQ = 1024
GROUP = 16


def draw_query_rows(key, part):
    noise_key = jax.random.fold_in(key, 11)
    shaped = (SEQ, QUERY_HEADS * HEAD_DIM)
    entries = jnp.clip(jax.random.normal(noise_key, shaped, jnp.float32), -4.5, 4.5)
    return entries.astype(jnp.bfloat16)


def draw_key_rows(key, part):
    noise_key = jax.random.fold_in(key, 13)
    shaped = (SEQ, KV_HEADS * HEAD_DIM)
    entries = jnp.clip(jax.random.normal(noise_key, shaped, jnp.float32), -4.5, 4.5)
    return entries.astype(jnp.bfloat16)


def draw_span_order(key, part):
    pair_key, flip_key = jax.random.split(jax.random.fold_in(key, 17))
    halves = SPANS // 2
    pairs = jax.random.permutation(pair_key, halves).astype(jnp.int32)
    flips = jax.random.randint(flip_key, (halves,), 0, 2)
    first_span = jnp.where(flips == 1, pairs, SPANS - 1 - pairs)
    second_span = SPANS - 1 - first_span
    return jnp.stack([first_span, second_span], axis=1).reshape(SPANS).astype(jnp.int32)


def level_of(rng, dims, cuts, least, largest):
    factor_of, own = 1.0, jax.random.fold_in(rng, 6)
    for position, parts in cuts:
        heights = jnp.exp(jax.random.uniform(jax.random.fold_in(own, position), (parts,), jnp.float32, least / len(cuts), largest / len(cuts)))
        factor_of = factor_of * jnp.repeat(heights, dims[position] // parts).reshape([-1 if axis == position else 1 for axis in range(len(dims))])
    return factor_of


def gaussian(stream_key, shape, scale, bound, shards=(), held_as=jnp.bfloat16):
    loudness = level_of(stream_key, shape, shards, -0.22, 0.18) if shards else 1.0
    values = jax.random.normal(stream_key, shape, jnp.float32) * scale * loudness
    return jnp.minimum(jnp.maximum(values, -bound), bound).astype(held_as)


def setup_inputs(seed: int = 0) -> dict:
    keys = jax.random.split(jax.random.key(seed), 6)
    query_rows = draw_query_rows(jax.random.fold_in(keys[5], 71), 0)
    key_rows = draw_key_rows(jax.random.fold_in(keys[5], 71), 0)
    value_rows = gaussian(keys[2], (SEQ, KV_HEADS * HEAD_DIM), 1.0, 6.0, ((0, 4),))
    out_grad = gaussian(keys[3], (SEQ, QUERY_HEADS * HEAD_DIM), 4.0, 16.0, ((0, 4), (1, 8)))
    span_order = draw_span_order(jax.random.fold_in(keys[5], 71), 0)
    return dict(query_rows=query_rows, key_rows=key_rows, value_rows=value_rows, out_grad=out_grad, span_order=span_order)


def reference(query_rows, key_rows, value_rows, out_grad, span_order):
    score_scale = 1.0 / math.sqrt(HEAD_DIM)
    positions = (span_order[:, None] * SPAN + jnp.arange(SPAN, dtype=jnp.int32)[None, :]).reshape(SEQ)
    visible = positions[None, :] <= positions[:, None]
    query_heads = query_rows.reshape(SEQ, QUERY_HEADS, HEAD_DIM).transpose(1, 0, 2)
    grad_heads = out_grad.reshape(SEQ, QUERY_HEADS, HEAD_DIM).transpose(1, 0, 2)
    key_heads = key_rows.reshape(SEQ, KV_HEADS, HEAD_DIM).transpose(1, 0, 2)
    value_heads = value_rows.reshape(SEQ, KV_HEADS, HEAD_DIM).transpose(1, 0, 2)

    def attend_head(head_id):
        kv_group = head_id // GROUP
        query_head = query_heads[head_id]
        grad_head = grad_heads[head_id]
        key_head = key_heads[kv_group]
        value_head = value_heads[kv_group]
        scores = jnp.dot(query_head, key_head.T, preferred_element_type=jnp.float32) * score_scale
        scores = jnp.where(visible, scores, -jnp.inf)
        row_top = lax.optimization_barrier(jnp.max(scores, axis=1, keepdims=True))
        log_total = row_top + jnp.log(lax.optimization_barrier(jnp.sum(jnp.exp(scores - row_top), axis=1, keepdims=True)))
        probs = jnp.exp(scores - log_total)
        probs_low = probs.astype(jnp.bfloat16)
        attended = jnp.dot(probs_low, value_head, preferred_element_type=jnp.float32).astype(jnp.bfloat16)
        row_dots = lax.optimization_barrier(jnp.sum(grad_head.astype(jnp.float32) * attended.astype(jnp.float32), axis=1, keepdims=True))
        prob_grad = jnp.dot(grad_head, value_head.T, preferred_element_type=jnp.float32)
        score_grad = (probs * (prob_grad - row_dots)).astype(jnp.bfloat16)
        query_grads = (jnp.dot(score_grad, key_head, preferred_element_type=jnp.float32) * score_scale).astype(jnp.bfloat16)
        key_part = jnp.dot(score_grad.T, query_head, preferred_element_type=jnp.float32) * score_scale
        value_part = jnp.dot(probs_low.T, grad_head, preferred_element_type=jnp.float32)
        return (attended, query_grads, key_part, value_part)
    attended, query_grads, key_parts, value_parts = lax.map(attend_head, jnp.arange(QUERY_HEADS, dtype=jnp.int32))
    attn_out = attended.transpose(1, 0, 2).reshape(SEQ, QUERY_HEADS * HEAD_DIM)
    query_grad = query_grads.transpose(1, 0, 2).reshape(SEQ, QUERY_HEADS * HEAD_DIM)
    key_sums = key_parts.reshape(KV_HEADS, GROUP, SEQ, HEAD_DIM).sum(axis=1)
    value_sums = value_parts.reshape(KV_HEADS, GROUP, SEQ, HEAD_DIM).sum(axis=1)
    key_grad = key_sums.transpose(1, 0, 2).reshape(SEQ, KV_HEADS * HEAD_DIM).astype(jnp.bfloat16)
    value_grad = value_sums.transpose(1, 0, 2).reshape(SEQ, KV_HEADS * HEAD_DIM).astype(jnp.bfloat16)
    return (attn_out, query_grad, key_grad, value_grad)
```

```python
import functools
import math

import jax
import jax.numpy as jnp
from jax import lax
from jax.experimental import pallas as pl
from jax.experimental.pallas import tpu as pltpu
from jax.sharding import PartitionSpec as P

KV_HEADS = 8
HEAD_DIM = 128
GROUP = 16
F32 = jnp.float32
BF16 = jnp.bfloat16


def dot_nn(a, b):
    return lax.dot_general(a, b, (((1,), (0,)), ((), ())), preferred_element_type=F32)


def dot_nt(a, b):
    return lax.dot_general(a, b, (((1,), (1,)), ((), ())), preferred_element_type=F32)


def attend_kernel(n_ctx, span, heads, meta, q_ref, g_ref, *rest):
    kv_refs = rest[:n_ctx]
    o_ref, dq_ref, dkv_ref = rest[n_ctx : n_ctx + 3]
    k_s, v_s, kt_s, vt_s, dk_s, dv_s, p_s = rest[n_ctx + 3 :]
    d = HEAD_DIM
    tile = 2 * span
    n_tiles = n_ctx + 1
    scale = 1.0 / math.sqrt(d)
    log2e_scale = scale * math.log2(math.e)
    step = pl.program_id(0)
    ctx = meta[2 * n_ctx]

    @pl.when(step == 0)
    def _():
        for r in range(n_ctx):
            src = lax.rem(ctx + r, n_ctx)
            for half in range(2):
                pos = meta[2 * src + half]
                rows = pl.ds(pl.multiple_of(pos * span, span), span)
                kv = kv_refs[r][half * span : (half + 1) * span, :]
                k_s[rows, :] = kv[:, :d]
                v_s[rows, :] = kv[:, d:]
        for t in range(n_ctx):
            rows = slice(t * tile, (t + 1) * tile)
            kt_s[t] = k_s[rows, :].astype(F32).T.astype(BF16)
            vt_s[t] = v_s[rows, :].astype(F32).T.astype(BF16)
        dk_s[...] = jnp.zeros_like(dk_s)
        dv_s[...] = jnp.zeros_like(dv_s)

    first, second = meta[2 * ctx], meta[2 * ctx + 1]
    hi, lo = jnp.maximum(first, second), jnp.minimum(first, second)
    hi_row = pl.multiple_of(jnp.where(first > second, 0, span), span)
    lo_row = pl.multiple_of(span - hi_row, span)
    hi_tiles = (hi + 2) // 2
    sure_hi = (n_ctx + 2) // 2

    def load(ref, row):
        return jnp.concatenate(
            [ref[pl.ds(row, span), h * d : (h + 1) * d] for h in range(heads)], axis=0
        )

    q = {True: load(q_ref, hi_row), False: load(q_ref, lo_row)}
    g = {True: load(g_ref, hi_row), False: load(g_ref, lo_row)}
    width = heads * span
    kinds, key_tiles, flags = [], [], []
    for t in range(n_tiles):
        if t < sure_hi:
            kinds.append(True)
            key_tiles.append(t)
            flags.append(None)
        elif t == n_tiles - 1:
            kinds.append(False)
            key_tiles.append(t - hi_tiles)
            flags.append(None)
        else:
            is_hi = t < hi_tiles
            kinds.append(None)
            key_tiles.append(jnp.where(is_hi, t, t - hi_tiles))
            flags.append(is_hi)

    def pick(t, pair):
        if kinds[t] is None:
            return jnp.where(flags[t], pair[True], pair[False])
        return pair[kinds[t]]

    def rows_of(t):
        kt = key_tiles[t]
        if isinstance(kt, int):
            return pl.ds(kt * tile, tile)
        return pl.ds(pl.multiple_of(kt * tile, tile), tile)

    row_of = {True: hi_row, False: lo_row}

    def operand(t, ref, pair):
        if kinds[t] is None:
            return load(ref, pl.multiple_of(pick(t, row_of), span))
        return pair[kinds[t]]

    diff = lax.broadcasted_iota(jnp.int32, (tile, width), 0) - lax.rem(
        lax.broadcasted_iota(jnp.int32, (tile, width), 1), span
    )
    qs = [operand(t, q_ref, q) for t in range(n_tiles)]
    gs = [operand(t, g_ref, g) for t in range(n_tiles)]

    tops = {True: None, False: None}

    def fold(acc, t, part, op, neutral):
        for kind in (True, False):
            if kinds[t] is None:
                use = flags[t] if kind else jnp.logical_not(flags[t])
                term = jnp.where(use, part, neutral)
            elif kinds[t] == kind:
                term = part
            else:
                continue
            acc[kind] = term if acc[kind] is None else op(acc[kind], term)

    for t in range(n_tiles):
        s = dot_nt(k_s[rows_of(t), :], qs[t])
        if t >= sure_hi - 1:
            limit = pick(t, {True: hi, False: lo}) * span - key_tiles[t] * tile
            s = jnp.where(diff <= limit, s, -jnp.inf)
        p_s[t] = s
        fold(tops, t, jnp.max(s, axis=0, keepdims=True), jnp.maximum, -jnp.inf)
    sums = {True: None, False: None}
    for t in range(n_tiles):
        p = jnp.exp2((p_s[t] - pick(t, tops)) * log2e_scale)
        p_s[t] = p
        fold(sums, t, jnp.sum(p, axis=0, keepdims=True), jnp.add, 0.0)
    inverse = {kind: 1.0 / sums[kind] for kind in (True, False)}
    outs = {True: None, False: None}
    for t in range(n_tiles):
        p = p_s[t] * pick(t, inverse)
        p_s[t] = p
        p_low = p.astype(BF16)
        fold(outs, t, dot_nn(vt_s[key_tiles[t]], p_low), jnp.add, 0.0)
        dv_s[rows_of(t), :] += dot_nn(p_low, gs[t])
    dots = {}
    for kind in (True, False):
        parts = []
        for h in range(heads):
            cols = slice(h * span, (h + 1) * span)
            o = outs[kind][:, cols].T.astype(BF16)
            o_ref[pl.ds(row_of[kind], span), h * d : (h + 1) * d] = o
            prod = g[kind][cols, :].astype(F32) * o.astype(F32)
            parts.append(jnp.sum(prod.T, axis=0, keepdims=True))
        dots[kind] = jnp.concatenate(parts, axis=1)
    dqs = {True: None, False: None}
    for t in range(n_tiles):
        dp = dot_nt(v_s[rows_of(t), :], gs[t])
        ds = (p_s[t] * (dp - pick(t, dots))).astype(BF16)
        fold(dqs, t, dot_nn(kt_s[key_tiles[t]], ds), jnp.add, 0.0)
        dk_s[rows_of(t), :] += dot_nn(ds, qs[t])
    for kind in (True, False):
        for h in range(heads):
            cols = slice(h * span, (h + 1) * span)
            dq = (dqs[kind][:, cols] * scale).T.astype(BF16)
            dq_ref[pl.ds(row_of[kind], span), h * d : (h + 1) * d] = dq

    @pl.when(step == pl.num_programs(0) - 1)
    def _():
        for i in range(2 * n_ctx):
            rows = pl.ds(pl.multiple_of(meta[i] * span, span), span)
            dkv_ref[i * span : (i + 1) * span, :d] = (dk_s[rows, :] * scale).astype(BF16)
            dkv_ref[i * span : (i + 1) * span, d:] = dv_s[rows, :].astype(BF16)


def attend(meta, q, g, kvs, n_ctx, heads):
    tokens, width = q.shape
    span = tokens // 2
    steps = width // (heads * HEAD_DIM)
    keys = tokens * n_ctx
    d = HEAD_DIM
    col = pl.BlockSpec((tokens, heads * d), lambda i, m: (0, i))
    whole = pl.BlockSpec((tokens, 2 * d), lambda i, m: (0, 0))
    flops = 6 * 2 * (width // d) * tokens // 2 * (n_ctx + 1) * tokens * d
    return pl.pallas_call(
        functools.partial(attend_kernel, n_ctx, span, heads),
        grid_spec=pltpu.PrefetchScalarGridSpec(
            num_scalar_prefetch=1,
            grid=(steps,),
            in_specs=[col, col] + [whole] * n_ctx,
            out_specs=[col, col, pl.BlockSpec((keys, 2 * d), lambda i, m: (0, 0))],
            scratch_shapes=[
                pltpu.VMEM((keys, d), BF16),
                pltpu.VMEM((keys, d), BF16),
                pltpu.VMEM((n_ctx, d, tokens), BF16),
                pltpu.VMEM((n_ctx, d, tokens), BF16),
                pltpu.VMEM((keys, d), F32),
                pltpu.VMEM((keys, d), F32),
                pltpu.VMEM((n_ctx + 1, tokens, heads * span), F32),
            ],
        ),
        out_shape=[
            jax.ShapeDtypeStruct(q.shape, BF16),
            jax.ShapeDtypeStruct(q.shape, BF16),
            jax.ShapeDtypeStruct((keys, 2 * d), BF16),
        ],
        cost_estimate=pl.CostEstimate(
            flops=flops, bytes_accessed=8 * q.size, transcendentals=0
        ),
        name="attend",
    )(meta, q, g, *kvs)


def total_kernel(x_ref, dk_ref, dv_ref):
    n_ctx, groups, replicas = x_ref.shape[:3]
    d = HEAD_DIM
    for k in range(groups):
        acc = None
        for c in range(n_ctx):
            for r in range(replicas):
                part = x_ref[c, k, r].astype(F32)
                acc = part if acc is None else acc + part
        dk_ref[:, k * d : (k + 1) * d] = acc[:, :d].astype(BF16)
        dv_ref[:, k * d : (k + 1) * d] = acc[:, d:].astype(BF16)


def total(x, rows_out):
    shape = jax.ShapeDtypeStruct((rows_out, KV_HEADS * HEAD_DIM), BF16)
    return pl.pallas_call(total_kernel, out_shape=[shape, shape], name="total")(x)


def per_device(query_rows, key_rows, value_rows, out_grad, span_order):
    n_ctx = lax.axis_size("ctx")
    n_head = lax.axis_size("head")
    tokens = query_rows.shape[0]
    q_heads = query_rows.shape[1] // HEAD_DIM
    rows_out = tokens // n_head
    replicas = n_head // KV_HEADS
    ctx_index = lax.axis_index("ctx")
    head_index = lax.axis_index("head")
    kv_group = head_index * q_heads // GROUP
    own = jnp.concatenate(
        [
            lax.dynamic_slice_in_dim(a, kv_group * HEAD_DIM, HEAD_DIM, 1)
            for a in (key_rows, value_rows)
        ],
        axis=1,
    )
    kvs = [own]
    for r in range(1, n_ctx):
        kvs.append(lax.ppermute(own, "ctx", [((i + r) % n_ctx, i) for i in range(n_ctx)]))
    meta = jnp.concatenate([span_order, ctx_index[None].astype(jnp.int32)])
    heads = math.gcd(q_heads, HEADS)
    attn_out, query_grad, partial = attend(meta, query_rows, out_grad, kvs, n_ctx, heads)
    parts = lax.all_to_all(
        partial.reshape(n_ctx * n_head, rows_out, 2 * HEAD_DIM),
        ("ctx", "head"),
        split_axis=0,
        concat_axis=0,
    )
    parts = parts.reshape(n_ctx, KV_HEADS, replicas, rows_out, 2 * HEAD_DIM)
    key_grad, value_grad = total(parts, rows_out)
    return (attn_out, query_grad, key_grad, value_grad)


HEADS = 4


def solution(mesh):
    in_specs = (P("ctx", "head"), P("ctx", None), P("ctx", None), P("ctx", "head"), P())
    out_specs = (
        P("ctx", "head"),
        P("ctx", "head"),
        P(("ctx", "head"), None),
        P(("ctx", "head"), None),
    )
    return jax.shard_map(
        per_device, mesh=mesh, in_specs=in_specs, out_specs=out_specs, check_vma=False
    )
```

```python
import functools
import math

import jax
import jax.numpy as jnp
from jax import lax
from jax.experimental import pallas as pl
from jax.experimental.pallas import tpu as pltpu
from jax.sharding import PartitionSpec as P


KV_HEADS = 8
HEAD_DIM = 128
GROUP = 16
HEADS = 8
VMEM_BYTES = 24 << 20
COVER = 20_000_000_000
F32 = jnp.float32
BF16 = jnp.bfloat16
SCALE = 1.0 / math.sqrt(HEAD_DIM)
EXP_SCALE = SCALE * math.log2(math.e)


def dot_nn(a, b):
    return lax.dot_general(a, b, (((1,), (0,)), ((), ())), preferred_element_type=F32)


def dot_nt(a, b):
    return lax.dot_general(a, b, (((1,), (1,)), ((), ())), preferred_element_type=F32)


def partner(ctx, r, n_ctx):
    return ctx ^ r if n_ctx & (n_ctx - 1) == 0 else (ctx + r) % n_ctx


class Plan:
    def __init__(self, n_ctx, span, meta):
        self.n_ctx, self.span, self.meta = n_ctx, span, meta
        self.tile = 2 * span
        self.slots = n_ctx + 1
        self.ctx = lax.axis_index("ctx")
        first, second = meta[2 * self.ctx], meta[2 * self.ctx + 1]
        self.hi, self.lo = jnp.maximum(first, second), jnp.minimum(first, second)
        hi_row = pl.multiple_of(jnp.where(first > second, 0, span), span)
        self.row = {True: hi_row, False: pl.multiple_of(span - hi_row, span)}
        self.hi_tiles = (self.hi + 2) // 2
        self.sure_hi = (n_ctx + 2) // 2

    def kind(self, t):
        if t < self.sure_hi:
            return True
        return False if t == self.slots - 1 else None

    def is_hi(self, t):
        return t < self.hi_tiles

    def key_tile(self, t):
        kind = self.kind(t)
        if kind:
            return t
        if kind is None:
            return jnp.where(self.is_hi(t), t, t - self.hi_tiles)
        return t - self.hi_tiles

    def keys(self, t):
        return pl.ds(pl.multiple_of(self.key_tile(t) * self.tile, self.tile), self.tile)

    def pick(self, t, pair):
        kind = self.kind(t)
        if kind is None:
            return jnp.where(self.is_hi(t), pair[True], pair[False])
        return pair[kind]

    def fold(self, acc, t, part, op, neutral):
        for kind in (True, False):
            if self.kind(t) is None:
                use = self.is_hi(t) if kind else jnp.logical_not(self.is_hi(t))
                term = jnp.where(use, part, neutral)
            elif self.kind(t) == kind:
                term = part
            else:
                continue
            acc[kind] = term if acc[kind] is None else op(acc[kind], term)

    def sort(self, shards, out):
        for r, shard in enumerate(shards):
            src = partner(self.ctx, r, self.n_ctx)
            for half in range(2):
                pos = self.meta[2 * src + half]
                rows = pl.ds(pl.multiple_of(pos * self.span, self.span), self.span)
                out[rows, :] = shard[half * self.span : (half + 1) * self.span, :]

    def unsort(self, total, outs):
        for r, out in enumerate(outs):
            dest = partner(self.ctx, r, self.n_ctx)
            for half in range(2):
                pos = self.meta[2 * dest + half]
                rows = pl.ds(pl.multiple_of(pos * self.span, self.span), self.span)
                out[half * self.span : (half + 1) * self.span, :] = total(rows)

    def queries(self, ref, row, cols):
        return jnp.concatenate(
            [
                ref[pl.ds(row, self.span), c : c + HEAD_DIM]
                for c in range(cols.start, cols.stop, HEAD_DIM)
            ],
            axis=0,
        )

    def slot_queries(self, ref, cols):
        pair = {k: self.queries(ref, self.row[k], cols) for k in (True, False)}
        out = []
        for t in range(self.slots):
            if self.kind(t) is None:
                row = pl.multiple_of(self.pick(t, self.row), self.span)
                out.append(self.queries(ref, row, cols))
            else:
                out.append(pair[self.kind(t)])
        return pair, out


def groups(width, heads):
    step = heads * HEAD_DIM
    return [slice(c, c + step) for c in range(0, width, step)]


def own_kernel(kv_ref, k_ref, v_ref):
    tokens = k_ref.shape[0]
    k_ref[...] = kv_ref[:tokens, :]
    v_ref[...] = kv_ref[tokens:, :]


def split_own(own):
    vmem = pl.BlockSpec(memory_space=pltpu.VMEM)
    shape = jax.ShapeDtypeStruct((own.shape[0] // 2, own.shape[1]), BF16)
    return pl.pallas_call(
        own_kernel,
        in_specs=[vmem],
        out_specs=[vmem, vmem],
        out_shape=[shape, shape],
        cost_estimate=pl.CostEstimate(flops=COVER, bytes_accessed=0, transcendentals=0),
        compiler_params=pltpu.CompilerParams(vmem_limit_bytes=VMEM_BYTES),
        name="own",
    )(own)


def forward_kernel(n_ctx, span, heads, meta, q_ref, g_ref, *rest):
    shards = rest[:n_ctx]
    p_ref, inv_ref, gs_ref, k_ref = rest[n_ctx : n_ctx + 4]
    dv_refs = rest[n_ctx + 4 : 2 * n_ctx + 4]
    s_ref, acc_ref = rest[2 * n_ctx + 4 :]
    plan = Plan(n_ctx, span, meta)
    d = HEAD_DIM
    plan.sort(shards, k_ref)
    acc_ref[...] = jnp.zeros_like(acc_ref)
    width = heads * span
    diff = lax.broadcasted_iota(jnp.int32, (plan.tile, width), 0) - lax.rem(
        lax.broadcasted_iota(jnp.int32, (plan.tile, width), 1), span
    )
    for cols in groups(q_ref.shape[1], heads):
        _, qs = plan.slot_queries(q_ref, cols)
        tops = {True: None, False: None}
        for t in range(plan.slots):
            s = dot_nt(k_ref[plan.keys(t), :], qs[t])
            if t >= plan.sure_hi - 1:
                position = plan.pick(t, {True: plan.hi, False: plan.lo})
                limit = position * span - plan.key_tile(t) * plan.tile
                s = jnp.where(diff <= limit, s, -jnp.inf)
            s_ref[t, :, cols] = s
            plan.fold(tops, t, jnp.max(s, axis=0, keepdims=True), jnp.maximum, -jnp.inf)
        sums = {True: None, False: None}
        for t in range(plan.slots):
            p = jnp.exp2((s_ref[t, :, cols] - plan.pick(t, tops)) * EXP_SCALE)
            p_ref[t, :, cols] = p.astype(BF16)
            plan.fold(sums, t, jnp.sum(p, axis=0, keepdims=True), jnp.add, 0.0)
        for kind, r in ((True, 0), (False, 1)):
            inverse = 1.0 / sums[kind]
            inv_ref[r : r + 1, cols] = inverse
            for h in range(heads):
                here = slice(cols.start + h * d, cols.start + (h + 1) * d)
                row = inverse[:, h * span : (h + 1) * span]
                column = jnp.broadcast_to(row, (span, span)).T
                g = g_ref[pl.ds(plan.row[kind], span), here].astype(F32)
                gs_ref[pl.ds(plan.row[kind], span), here] = (g * column).astype(BF16)
        _, gs = plan.slot_queries(gs_ref, cols)
        for t in range(plan.slots):
            acc_ref[plan.keys(t), :] += dot_nn(p_ref[t, :, cols], gs[t])
    plan.unsort(lambda rows: acc_ref[rows, :].astype(BF16), dv_refs)


def backward_kernel(n_ctx, span, heads, meta, p_ref, inv_ref, gs_ref, q_ref, *rest):
    shards = rest[:n_ctx]
    o_ref, ds_ref = rest[n_ctx : n_ctx + 2]
    dk_refs = rest[n_ctx + 2 : 2 * n_ctx + 2]
    v_ref, vt_ref, acc_ref = rest[2 * n_ctx + 2 :]
    plan = Plan(n_ctx, span, meta)
    d = HEAD_DIM
    plan.sort(shards, v_ref)
    for t in range(n_ctx):
        vt_ref[t] = v_ref[t * plan.tile : (t + 1) * plan.tile, :].astype(F32).T.astype(BF16)
    acc_ref[...] = jnp.zeros_like(acc_ref)
    for cols in groups(q_ref.shape[1], heads):
        _, qs = plan.slot_queries(q_ref, cols)
        _, gs = plan.slot_queries(gs_ref, cols)
        outs = {True: None, False: None}
        for t in range(plan.slots):
            part = dot_nn(vt_ref[plan.key_tile(t)], p_ref[t, :, cols])
            plan.fold(outs, t, part, jnp.add, 0.0)
        dots = {}
        for kind, r in ((True, 0), (False, 1)):
            out = outs[kind] * inv_ref[r : r + 1, cols]
            parts = []
            for h in range(heads):
                here = slice(cols.start + h * d, cols.start + (h + 1) * d)
                o = out[:, h * span : (h + 1) * span].T.astype(BF16)
                o_ref[pl.ds(plan.row[kind], span), here] = o
                g = gs_ref[pl.ds(plan.row[kind], span), here].astype(F32)
                parts.append(jnp.sum((g * o.astype(F32)).T, axis=0, keepdims=True))
            dots[kind] = jnp.concatenate(parts, axis=1)
        for t in range(plan.slots):
            dp = dot_nt(v_ref[plan.keys(t), :], gs[t])
            ds = (p_ref[t, :, cols].astype(F32) * (dp - plan.pick(t, dots))).astype(BF16)
            ds_ref[t, :, cols] = ds
            acc_ref[plan.keys(t), :] += dot_nn(ds, qs[t])
    plan.unsort(lambda rows: (acc_ref[rows, :] * SCALE).astype(BF16), dk_refs)


def query_kernel(n_ctx, span, heads, meta, ds_ref, k_ref, dq_ref, kt_ref):
    plan = Plan(n_ctx, span, meta)
    d = HEAD_DIM
    for t in range(n_ctx):
        kt_ref[t] = k_ref[t * plan.tile : (t + 1) * plan.tile, :].astype(F32).T.astype(BF16)
    for cols in groups(dq_ref.shape[1], heads):
        dqs = {True: None, False: None}
        for t in range(plan.slots):
            part = dot_nn(kt_ref[plan.key_tile(t)], ds_ref[t, :, cols])
            plan.fold(dqs, t, part, jnp.add, 0.0)
        for kind in (True, False):
            for h in range(heads):
                here = slice(cols.start + h * d, cols.start + (h + 1) * d)
                dq = (dqs[kind][:, h * span : (h + 1) * span] * SCALE).T.astype(BF16)
                dq_ref[pl.ds(plan.row[kind], span), here] = dq


def call(body, out_shape, scratch, flops):
    vmem = pl.BlockSpec(memory_space=pltpu.VMEM)

    def run(meta, *args):
        return pl.pallas_call(
            body,
            in_specs=[pl.BlockSpec(memory_space=pltpu.SMEM)] + [vmem] * len(args),
            out_specs=[vmem] * len(out_shape),
            out_shape=out_shape,
            scratch_shapes=scratch,
            cost_estimate=pl.CostEstimate(
                flops=flops, bytes_accessed=flops // 512, transcendentals=0
            ),
            compiler_params=pltpu.CompilerParams(vmem_limit_bytes=VMEM_BYTES),
        )(meta, *args)

    return run


def per_device(query_rows, key_rows, value_rows, out_grad, span_order):
    n_ctx = lax.axis_size("ctx")
    n_head = lax.axis_size("head")
    tokens, width = query_rows.shape
    span = tokens // 2
    keys = tokens * n_ctx
    d = HEAD_DIM
    q_heads = width // d
    rows_out = tokens // n_head
    replicas = n_head // KV_HEADS
    heads = math.gcd(q_heads, HEADS)

    def shift(a, r, back=False):
        pairs = [(partner(i, r, n_ctx), i) for i in range(n_ctx)]
        return lax.ppermute(a, "ctx", [p[::-1] for p in pairs] if back else pairs)

    def shape(dims, dtype=BF16):
        return jax.ShapeDtypeStruct(dims, dtype)

    others = range(1, n_ctx)
    kv_group = lax.axis_index("head") * q_heads // GROUP
    own = lax.optimization_barrier(
        jnp.concatenate(
            [lax.dynamic_slice_in_dim(a, kv_group * d, d, 1) for a in (key_rows, value_rows)]
        )
    )
    key_own, value_own = split_own(own)

    def gather(own, name):
        if n_ctx != 4 or name == "value":
            return [own] + [shift(own, r) for r in others]
        near, far = shift(own, 1), shift(own, 2)
        across = lax.ppermute(far, "ctx", [(i ^ 1, i) for i in range(n_ctx)])
        return [own, near, far, across]

    key_shards, value_shards = gather(key_own, "key"), gather(value_own, "value")
    slots = (n_ctx + 1, tokens, q_heads * span)
    rows, pair, shard = shape((tokens, width)), shape((2, q_heads * span), F32), shape((tokens, d))
    work = 2 * slots[0] * slots[1] * slots[2] * d
    bind = lambda f: functools.partial(f, n_ctx, span, heads)
    p, inverse, grads, key_sorted, *value_parts = call(
        bind(forward_kernel),
        [shape(slots), pair, rows, shape((keys, d))] + [shard] * n_ctx,
        [pltpu.VMEM(slots, F32), pltpu.VMEM((keys, d), F32)], 2 * work,
    )(span_order, query_rows, out_grad, *key_shards)
    attn_out, score_grads, *key_parts = call(
        bind(backward_kernel), [rows, shape(slots)] + [shard] * n_ctx,
        [
            pltpu.VMEM((keys, d), BF16),
            pltpu.VMEM((n_ctx, d, tokens), BF16),
            pltpu.VMEM((keys, d), F32),
        ], 3 * work,
    )(span_order, p, inverse, grads, query_rows, *value_shards)
    (query_grad,) = call(
        bind(query_kernel), [rows],
        [pltpu.VMEM((n_ctx, d, tokens), BF16)], work,
    )(span_order, score_grads, key_sorted)

    def scatter(parts, name):
        if n_ctx == 4 and name == "value_grad":
            given = jnp.concatenate([parts[1], parts[3]])
            taken = shift(given, 1).astype(F32)
            far = (parts[2].astype(F32) + taken[tokens:]).astype(BF16)
            far = shift(far, 2).astype(F32)
            return (parts[0].astype(F32) + taken[:tokens] + far).astype(BF16)
        total = parts[0].astype(F32)
        for r in others:
            total += shift(parts[r], r, True).astype(F32)
        return total.astype(BF16)

    value_sum, key_sum = scatter(value_parts, "value_grad"), scatter(key_parts, "key_grad")
    owned = jnp.concatenate([key_sum, value_sum], axis=1)
    parts = lax.all_to_all(
        owned.reshape(n_head, rows_out, 2 * d), "head", split_axis=0, concat_axis=0
    )
    key_grad, value_grad = total(parts.reshape(KV_HEADS, replicas, rows_out, 2 * d), rows_out)
    return (attn_out, query_grad, key_grad, value_grad)


def total_kernel(x_ref, dk_ref, dv_ref):
    d = HEAD_DIM
    for k in range(x_ref.shape[0]):
        acc = x_ref[k, 0].astype(F32)
        for r in range(1, x_ref.shape[1]):
            acc += x_ref[k, r].astype(F32)
        dk_ref[:, k * d : (k + 1) * d] = acc[:, :d].astype(BF16)
        dv_ref[:, k * d : (k + 1) * d] = acc[:, d:].astype(BF16)


def total(x, rows_out):
    shape = jax.ShapeDtypeStruct((rows_out, KV_HEADS * HEAD_DIM), BF16)
    return pl.pallas_call(
        total_kernel,
        out_shape=[shape, shape],
        compiler_params=pltpu.CompilerParams(vmem_limit_bytes=VMEM_BYTES),
        name="total",
    )(x)


def solution(mesh):
    in_specs = (P("ctx", "head"), P("ctx", None), P("ctx", None), P("ctx", "head"), P())
    out_specs = (
        P("ctx", "head"),
        P("ctx", "head"),
        P(("ctx", "head"), None),
        P(("ctx", "head"), None),
    )

    return jax.shard_map(
        per_device, mesh=mesh, in_specs=in_specs, out_specs=out_specs, check_vma=False
    )
```

```python
import functools
import math

import jax
import jax.numpy as jnp
from jax import lax
from jax.experimental import pallas as pl
from jax.experimental.pallas import tpu as pltpu
from jax.sharding import PartitionSpec as P


KV_HEADS = 8
HEAD_DIM = 128
GROUP = 16
HEADS = 8
VMEM_BYTES = 24 << 20
COVER = 20_000_000_000
F32 = jnp.float32
BF16 = jnp.bfloat16
SCALE = 1.0 / math.sqrt(HEAD_DIM)
EXP_SCALE = SCALE * math.log2(math.e)


def dot_nn(a, b):
    return lax.dot_general(a, b, (((1,), (0,)), ((), ())), preferred_element_type=F32)


def dot_nt(a, b):
    return lax.dot_general(a, b, (((1,), (1,)), ((), ())), preferred_element_type=F32)


def partner(ctx, r, n_ctx):
    return ctx ^ r if n_ctx & (n_ctx - 1) == 0 else (ctx + r) % n_ctx


class Plan:
    def __init__(self, n_ctx, span, meta):
        self.n_ctx, self.span = n_ctx, span
        self.tile = 2 * span
        self.slots = n_ctx + 1
        self.ctx = lax.axis_index("ctx")
        table = meta[...]
        self.order = [table[0, i] for i in range(2 * n_ctx)]
        first, second = self.position(self.ctx, 0), self.position(self.ctx, 1)
        self.hi, self.lo = jnp.maximum(first, second), jnp.minimum(first, second)
        hi_row = pl.multiple_of(jnp.where(first > second, 0, span), span)
        self.row = {True: hi_row, False: pl.multiple_of(span - hi_row, span)}
        self.hi_tiles = (self.hi + 2) // 2
        self.sure_hi = (n_ctx + 2) // 2

    def position(self, ctx, half):
        out = self.order[half]
        for c in range(1, self.n_ctx):
            out = jnp.where(ctx == c, self.order[2 * c + half], out)
        return out

    def kind(self, t):
        if t < self.sure_hi:
            return True
        return False if t == self.slots - 1 else None

    def is_hi(self, t):
        return t < self.hi_tiles

    def key_tile(self, t):
        kind = self.kind(t)
        if kind:
            return t
        if kind is None:
            return jnp.where(self.is_hi(t), t, t - self.hi_tiles)
        return t - self.hi_tiles

    def keys(self, t):
        return pl.ds(pl.multiple_of(self.key_tile(t) * self.tile, self.tile), self.tile)

    def pick(self, t, pair):
        kind = self.kind(t)
        if kind is None:
            return jnp.where(self.is_hi(t), pair[True], pair[False])
        return pair[kind]

    def fold(self, acc, t, part, op, neutral):
        for kind in (True, False):
            if self.kind(t) is None:
                use = self.is_hi(t) if kind else jnp.logical_not(self.is_hi(t))
                term = jnp.where(use, part, neutral)
            elif self.kind(t) == kind:
                term = part
            else:
                continue
            acc[kind] = term if acc[kind] is None else op(acc[kind], term)

    def sort(self, shards, out):
        for r, shard in enumerate(shards):
            src = partner(self.ctx, r, self.n_ctx)
            for half in range(2):
                pos = self.position(src, half)
                rows = pl.ds(pl.multiple_of(pos * self.span, self.span), self.span)
                out[rows, :] = shard[half * self.span : (half + 1) * self.span, :]

    def unsort(self, total, outs):
        for r, out in enumerate(outs):
            dest = partner(self.ctx, r, self.n_ctx)
            for half in range(2):
                pos = self.position(dest, half)
                rows = pl.ds(pl.multiple_of(pos * self.span, self.span), self.span)
                out[half * self.span : (half + 1) * self.span, :] = total(rows)

    def queries(self, ref, row, cols):
        return jnp.concatenate(
            [
                ref[pl.ds(row, self.span), c : c + HEAD_DIM]
                for c in range(cols.start, cols.stop, HEAD_DIM)
            ],
            axis=0,
        )

    def slot_queries(self, ref, cols):
        pair = {k: self.queries(ref, self.row[k], cols) for k in (True, False)}
        out = []
        for t in range(self.slots):
            if self.kind(t) is None:
                row = pl.multiple_of(self.pick(t, self.row), self.span)
                out.append(self.queries(ref, row, cols))
            else:
                out.append(pair[self.kind(t)])
        return pair, out


def pipeline(stages, parts):
    states = [{} for _ in parts]
    for step in range(len(parts) + len(stages) - 1):
        running = [
            stage(parts[step - k], states[step - k])
            for k, stage in reversed(list(enumerate(stages)))
            if 0 <= step - k < len(parts)
        ]
        while running:
            running = [r for r in running if next(r, running) is not running]


def groups(width, heads):
    step = heads * HEAD_DIM
    return [slice(c, c + step) for c in range(0, width, step)]


def own_kernel(kv_ref, k_ref, v_ref):
    tokens = k_ref.shape[0]
    k_ref[...] = kv_ref[:tokens, :]
    v_ref[...] = kv_ref[tokens:, :]


def split_own(own):
    vmem = pl.BlockSpec(memory_space=pltpu.VMEM)
    shape = jax.ShapeDtypeStruct((own.shape[0] // 2, own.shape[1]), BF16)
    return pl.pallas_call(
        own_kernel,
        in_specs=[vmem],
        out_specs=[vmem, vmem],
        out_shape=[shape, shape],
        cost_estimate=pl.CostEstimate(flops=COVER, bytes_accessed=0, transcendentals=0),
        compiler_params=pltpu.CompilerParams(vmem_limit_bytes=VMEM_BYTES),
        name="own",
    )(own)


def forward_kernel(n_ctx, span, heads, meta, q_ref, g_ref, *rest):
    shards = rest[:n_ctx]
    p_ref, inv_ref, gs_ref, k_ref = rest[n_ctx : n_ctx + 4]
    dv_refs = rest[n_ctx + 4 : 2 * n_ctx + 4]
    s_ref, acc_ref = rest[2 * n_ctx + 4 :]
    plan = Plan(n_ctx, span, meta)
    d = HEAD_DIM
    plan.sort(shards, k_ref)
    acc_ref[...] = jnp.zeros_like(acc_ref)
    width = heads * span
    diff = lax.broadcasted_iota(jnp.int32, (plan.tile, width), 0) - lax.rem(
        lax.broadcasted_iota(jnp.int32, (plan.tile, width), 1), span
    )

    def score(cols, state):
        state["tops"] = tops = {True: None, False: None}
        _, qs = plan.slot_queries(q_ref, cols)
        for t in range(plan.slots):
            s = dot_nt(k_ref[plan.keys(t), :], qs[t])
            if t >= plan.sure_hi - 1:
                position = plan.pick(t, {True: plan.hi, False: plan.lo})
                limit = position * span - plan.key_tile(t) * plan.tile
                s = jnp.where(diff <= limit, s, -jnp.inf)
            s_ref[t, :, cols] = s
            plan.fold(tops, t, jnp.max(s, axis=0, keepdims=True), jnp.maximum, -jnp.inf)
            yield

    def exponent(cols, state):
        tops = state["tops"]
        sums = {True: None, False: None}
        for t in range(plan.slots):
            p = jnp.exp2((s_ref[t, :, cols] - plan.pick(t, tops)) * EXP_SCALE)
            p_ref[t, :, cols] = p.astype(BF16)
            plan.fold(sums, t, jnp.sum(p, axis=0, keepdims=True), jnp.add, 0.0)
            yield
        for kind, r in ((True, 0), (False, 1)):
            inverse = 1.0 / sums[kind]
            inv_ref[r : r + 1, cols] = inverse
            for h in range(heads):
                here = slice(cols.start + h * d, cols.start + (h + 1) * d)
                row = inverse[:, h * span : (h + 1) * span]
                column = jnp.broadcast_to(row, (span, span)).T
                g = g_ref[pl.ds(plan.row[kind], span), here].astype(F32)
                gs_ref[pl.ds(plan.row[kind], span), here] = (g * column).astype(BF16)

    def value(cols, state):
        _, gs = plan.slot_queries(gs_ref, cols)
        for t in range(plan.slots):
            acc_ref[plan.keys(t), :] += dot_nn(p_ref[t, :, cols], gs[t])
            yield

    pipeline((score, exponent, value), groups(q_ref.shape[1], heads))
    plan.unsort(lambda rows: acc_ref[rows, :].astype(BF16), dv_refs)


def backward_kernel(n_ctx, span, heads, meta, p_ref, inv_ref, gs_ref, q_ref, *rest):
    shards = rest[:n_ctx]
    o_ref, ds_ref = rest[n_ctx : n_ctx + 2]
    dk_refs = rest[n_ctx + 2 : 2 * n_ctx + 2]
    v_ref, vt_ref, acc_ref = rest[2 * n_ctx + 2 :]
    plan = Plan(n_ctx, span, meta)
    d = HEAD_DIM
    plan.sort(shards, v_ref)
    for t in range(n_ctx):
        vt_ref[t] = v_ref[t * plan.tile : (t + 1) * plan.tile, :].astype(F32).T.astype(BF16)
    acc_ref[...] = jnp.zeros_like(acc_ref)

    def output(cols, state):
        outs = {True: None, False: None}
        for t in range(plan.slots):
            part = dot_nn(vt_ref[plan.key_tile(t)], p_ref[t, :, cols])
            plan.fold(outs, t, part, jnp.add, 0.0)
            yield
        state["dots"] = dots = {}
        for kind, r in ((True, 0), (False, 1)):
            out = outs[kind] * inv_ref[r : r + 1, cols]
            parts = []
            for h in range(heads):
                here = slice(cols.start + h * d, cols.start + (h + 1) * d)
                o = out[:, h * span : (h + 1) * span].T.astype(BF16)
                o_ref[pl.ds(plan.row[kind], span), here] = o
                g = gs_ref[pl.ds(plan.row[kind], span), here].astype(F32)
                parts.append(jnp.sum((g * o.astype(F32)).T, axis=0, keepdims=True))
            dots[kind] = jnp.concatenate(parts, axis=1)

    def score_grad(cols, state):
        _, qs = plan.slot_queries(q_ref, cols)
        _, gs = plan.slot_queries(gs_ref, cols)
        for t in range(plan.slots):
            dp = dot_nt(v_ref[plan.keys(t), :], gs[t])
            dots = plan.pick(t, state["dots"])
            ds = (p_ref[t, :, cols].astype(F32) * (dp - dots)).astype(BF16)
            ds_ref[t, :, cols] = ds
            acc_ref[plan.keys(t), :] += dot_nn(ds, qs[t])
            yield

    pipeline((output, score_grad), groups(q_ref.shape[1], heads))
    plan.unsort(lambda rows: (acc_ref[rows, :] * SCALE).astype(BF16), dk_refs)


def query_kernel(n_ctx, span, heads, meta, ds_ref, k_ref, dq_ref, kt_ref):
    plan = Plan(n_ctx, span, meta)
    d = HEAD_DIM
    for t in range(n_ctx):
        kt_ref[t] = k_ref[t * plan.tile : (t + 1) * plan.tile, :].astype(F32).T.astype(BF16)
    for cols in groups(dq_ref.shape[1], heads):
        dqs = {True: None, False: None}
        for t in range(plan.slots):
            part = dot_nn(kt_ref[plan.key_tile(t)], ds_ref[t, :, cols])
            plan.fold(dqs, t, part, jnp.add, 0.0)
        for kind in (True, False):
            for h in range(heads):
                here = slice(cols.start + h * d, cols.start + (h + 1) * d)
                dq = (dqs[kind][:, h * span : (h + 1) * span] * SCALE).T.astype(BF16)
                dq_ref[pl.ds(plan.row[kind], span), here] = dq


def call(body, out_shape, scratch, flops):
    vmem = pl.BlockSpec(memory_space=pltpu.VMEM)

    def run(meta, *args):
        return pl.pallas_call(
            body,
            in_specs=[vmem] * (1 + len(args)),
            out_specs=[vmem] * len(out_shape),
            out_shape=out_shape,
            scratch_shapes=scratch,
            cost_estimate=pl.CostEstimate(
                flops=flops, bytes_accessed=flops // 512, transcendentals=0
            ),
            compiler_params=pltpu.CompilerParams(vmem_limit_bytes=VMEM_BYTES),
        )(meta, *args)

    return run


def per_device(query_rows, key_rows, value_rows, out_grad, span_order):
    n_ctx = lax.axis_size("ctx")
    n_head = lax.axis_size("head")
    tokens, width = query_rows.shape
    span = tokens // 2
    keys = tokens * n_ctx
    d = HEAD_DIM
    q_heads = width // d
    rows_out = tokens // n_head
    replicas = n_head // KV_HEADS
    heads = math.gcd(q_heads, HEADS)

    def shift(a, r, back=False):
        pairs = [(partner(i, r, n_ctx), i) for i in range(n_ctx)]
        return lax.ppermute(a, "ctx", [p[::-1] for p in pairs] if back else pairs)

    def shape(dims, dtype=BF16):
        return jax.ShapeDtypeStruct(dims, dtype)

    others = range(1, n_ctx)
    order = span_order.reshape(1, 2 * n_ctx)
    kv_group = lax.axis_index("head") * q_heads // GROUP
    own = lax.optimization_barrier(
        jnp.concatenate(
            [lax.dynamic_slice_in_dim(a, kv_group * d, d, 1) for a in (key_rows, value_rows)]
        )
    )
    key_own, value_own = split_own(own)

    def gather(own, name):
        if n_ctx != 4 or name == "value":
            return [own] + [shift(own, r) for r in others]
        near, far = shift(own, 1), shift(own, 2)
        across = lax.ppermute(far, "ctx", [(i ^ 1, i) for i in range(n_ctx)])
        return [own, near, far, across]

    key_shards, value_shards = gather(key_own, "key"), gather(value_own, "value")
    slots = (n_ctx + 1, tokens, q_heads * span)
    rows, pair, shard = shape((tokens, width)), shape((2, q_heads * span), F32), shape((tokens, d))
    work = 2 * slots[0] * slots[1] * slots[2] * d
    bind = lambda f: functools.partial(f, n_ctx, span, heads)
    p, inverse, grads, key_sorted, *value_parts = call(
        bind(forward_kernel),
        [shape(slots), pair, rows, shape((keys, d))] + [shard] * n_ctx,
        [pltpu.VMEM(slots, F32), pltpu.VMEM((keys, d), F32)], 2 * work,
    )(order, query_rows, out_grad, *key_shards)
    attn_out, score_grads, *key_parts = call(
        bind(backward_kernel), [rows, shape(slots)] + [shard] * n_ctx,
        [
            pltpu.VMEM((keys, d), BF16),
            pltpu.VMEM((n_ctx, d, tokens), BF16),
            pltpu.VMEM((keys, d), F32),
        ], 3 * work,
    )(order, p, inverse, grads, query_rows, *value_shards)
    (query_grad,) = call(
        bind(query_kernel), [rows],
        [pltpu.VMEM((n_ctx, d, tokens), BF16)], work,
    )(order, score_grads, key_sorted)

    def plus(*parts):
        return functools.reduce(jnp.add, [a.astype(F32) for a in parts])

    if n_ctx == 4:
        far = shift(jnp.concatenate(value_parts[2:]), 2)
        near = plus(value_parts[1], far[tokens:]).astype(BF16)
        near = shift(jnp.concatenate([near, key_parts[1]]), 1)
        value_sum = plus(value_parts[0], far[:tokens], near[:tokens])
        key_sum = plus(key_parts[0], near[tokens:], *[shift(key_parts[r], r) for r in (2, 3)])
    else:
        value_sum, key_sum = [
            plus(parts[0], *[shift(parts[r], r, True) for r in others])
            for parts in (value_parts, key_parts)
        ]
    key_sum, value_sum = key_sum.astype(BF16), value_sum.astype(BF16)
    owned = jnp.concatenate([key_sum, value_sum], axis=1)
    parts = lax.all_to_all(
        owned.reshape(n_head, rows_out, 2 * d), "head", split_axis=0, concat_axis=0
    )
    key_grad, value_grad = total(parts.reshape(KV_HEADS, replicas, rows_out, 2 * d), rows_out)
    return (attn_out, query_grad, key_grad, value_grad)


def total_kernel(x_ref, dk_ref, dv_ref):
    d = HEAD_DIM
    for k in range(x_ref.shape[0]):
        acc = x_ref[k, 0].astype(F32)
        for r in range(1, x_ref.shape[1]):
            acc += x_ref[k, r].astype(F32)
        dk_ref[:, k * d : (k + 1) * d] = acc[:, :d].astype(BF16)
        dv_ref[:, k * d : (k + 1) * d] = acc[:, d:].astype(BF16)


def total(x, rows_out):
    shape = jax.ShapeDtypeStruct((rows_out, KV_HEADS * HEAD_DIM), BF16)
    return pl.pallas_call(
        total_kernel,
        out_shape=[shape, shape],
        compiler_params=pltpu.CompilerParams(vmem_limit_bytes=VMEM_BYTES),
        name="total",
    )(x)


def solution(mesh):
    in_specs = (P("ctx", "head"), P("ctx", None), P("ctx", None), P("ctx", "head"), P())
    out_specs = (
        P("ctx", "head"),
        P("ctx", "head"),
        P(("ctx", "head"), None),
        P(("ctx", "head"), None),
    )

    return jax.shard_map(
        per_device, mesh=mesh, in_specs=in_specs, out_specs=out_specs, check_vma=False
    )
```

```python
import functools
import math

import jax
import jax.numpy as jnp
from jax import lax
from jax.experimental import pallas as pl
from jax.experimental.pallas import tpu as pltpu
from jax.sharding import PartitionSpec as P


KV_HEADS = 8
HEAD_DIM = 128
GROUP = 16
HEADS = 8
VMEM_BYTES = 24 << 20
COVER = 20_000_000_000
F32 = jnp.float32
BF16 = jnp.bfloat16
SCALE = 1.0 / math.sqrt(HEAD_DIM)
EXP_SCALE = SCALE * math.log2(math.e)


def dot_nn(a, b):
    return lax.dot_general(a, b, (((1,), (0,)), ((), ())), preferred_element_type=F32)


def dot_nt(a, b):
    return lax.dot_general(a, b, (((1,), (1,)), ((), ())), preferred_element_type=F32)


def partner(ctx, r, n_ctx):
    return ctx ^ r if n_ctx & (n_ctx - 1) == 0 else (ctx + r) % n_ctx


class Plan:
    def __init__(self, n_ctx, span, meta):
        self.n_ctx, self.span = n_ctx, span
        self.tile = 2 * span
        self.slots = n_ctx + 1
        self.ctx = lax.axis_index("ctx")
        table = meta[...]
        self.order = [table[0, i] for i in range(2 * n_ctx)]
        first, second = self.position(self.ctx, 0), self.position(self.ctx, 1)
        self.hi, self.lo = jnp.maximum(first, second), jnp.minimum(first, second)
        hi_row = pl.multiple_of(jnp.where(first > second, 0, span), span)
        self.row = {True: hi_row, False: pl.multiple_of(span - hi_row, span)}
        self.hi_tiles = (self.hi + 2) // 2
        self.sure_hi = (n_ctx + 2) // 2

    def position(self, ctx, half):
        out = self.order[half]
        for c in range(1, self.n_ctx):
            out = jnp.where(ctx == c, self.order[2 * c + half], out)
        return out

    def kind(self, t):
        if t < self.sure_hi:
            return True
        return False if t == self.slots - 1 else None

    def is_hi(self, t):
        return t < self.hi_tiles

    def key_tile(self, t):
        kind = self.kind(t)
        if kind:
            return t
        if kind is None:
            return jnp.where(self.is_hi(t), t, t - self.hi_tiles)
        return t - self.hi_tiles

    def keys(self, t):
        return pl.ds(pl.multiple_of(self.key_tile(t) * self.tile, self.tile), self.tile)

    def pick(self, t, pair):
        kind = self.kind(t)
        if kind is None:
            return jnp.where(self.is_hi(t), pair[True], pair[False])
        return pair[kind]

    def fold(self, acc, t, part, op, neutral):
        for kind in (True, False):
            if self.kind(t) is None:
                use = self.is_hi(t) if kind else jnp.logical_not(self.is_hi(t))
                term = jnp.where(use, part, neutral)
            elif self.kind(t) == kind:
                term = part
            else:
                continue
            acc[kind] = term if acc[kind] is None else op(acc[kind], term)

    def sort(self, shards, out):
        for r, shard in enumerate(shards):
            src = partner(self.ctx, r, self.n_ctx)
            for half in range(2):
                pos = self.position(src, half)
                rows = pl.ds(pl.multiple_of(pos * self.span, self.span), self.span)
                out[rows, :] = shard[half * self.span : (half + 1) * self.span, :]

    def unsort(self, acc, outs, scale):
        for r, out in enumerate(outs):
            dest = partner(self.ctx, r, self.n_ctx)
            for half in range(2):
                block = acc[self.position(dest, half)] * scale
                out[half * self.span : (half + 1) * self.span, :] = block.T.astype(BF16)

    def side(self, t):
        return self.pick(t, {True: 0, False: 1})

    def add(self, acc, t, part):
        block = 2 * self.key_tile(t)
        acc[block] += part[:, : self.span]
        acc[block + 1] += part[:, self.span :]


def pipeline(stages, parts):
    states = [{} for _ in parts]
    for step in range(len(parts) + len(stages) - 1):
        running = [
            stage(parts[step - k], states[step - k])
            for k, stage in reversed(list(enumerate(stages)))
            if 0 <= step - k < len(parts)
        ]
        while running:
            running = [r for r in running if next(r, running) is not running]


def groups(width, heads):
    step = heads * HEAD_DIM
    return [slice(c, c + step) for c in range(0, width, step)]


def own_kernel(kv_ref, k_ref, v_ref):
    tokens = k_ref.shape[0]
    k_ref[...] = kv_ref[:tokens, :]
    v_ref[...] = kv_ref[tokens:, :]


def split_own(own):
    vmem = pl.BlockSpec(memory_space=pltpu.VMEM)
    shape = jax.ShapeDtypeStruct((own.shape[0] // 2, own.shape[1]), BF16)
    return pl.pallas_call(
        own_kernel,
        in_specs=[vmem],
        out_specs=[vmem, vmem],
        out_shape=[shape, shape],
        cost_estimate=pl.CostEstimate(flops=COVER, bytes_accessed=0, transcendentals=0),
        compiler_params=pltpu.CompilerParams(vmem_limit_bytes=VMEM_BYTES),
        name="own",
    )(own)


def prepare_kernel(n_ctx, span, heads, meta, q_ref, g_ref, qt_ref, gt_ref):
    plan = Plan(n_ctx, span, meta)
    d = HEAD_DIM
    for src, dst in ((q_ref, qt_ref), (g_ref, gt_ref)):
        for kind, side in ((True, 0), (False, 1)):
            for h in range(src.shape[1] // d):
                block = src[pl.ds(plan.row[kind], span), h * d : (h + 1) * d]
                dst[side, :, h * span : (h + 1) * span] = block.astype(F32).T.astype(BF16)


def forward_kernel(n_ctx, span, heads, meta, qt_ref, gt_ref, *rest):
    shards = rest[:n_ctx]
    p_ref, inv_ref, gs_ref, k_ref = rest[n_ctx : n_ctx + 4]
    dv_refs = rest[n_ctx + 4 : 2 * n_ctx + 4]
    acc_ref, limit_ref = rest[2 * n_ctx + 4 :]
    plan = Plan(n_ctx, span, meta)
    plan.sort(shards, k_ref)
    acc_ref[...] = jnp.zeros_like(acc_ref)
    first_masked = plan.sure_hi - 1
    dims = (plan.tile, span)
    diff = lax.broadcasted_iota(jnp.int32, dims, 0) - lax.broadcasted_iota(jnp.int32, dims, 1)
    for t in range(first_masked, plan.slots):
        position = plan.pick(t, {True: plan.hi, False: plan.lo})
        seen = diff <= position * span - plan.key_tile(t) * plan.tile
        limit_ref[t - first_masked] = jnp.where(seen, jnp.inf, -jnp.inf)

    def rows_of_eight(x):
        return x.reshape(x.shape[0] // 8, 8, x.shape[1])

    def score(cols, state):
        state["tops"] = tops = {True: None, False: None}
        for t in range(plan.slots):
            s = dot_nn(k_ref[plan.keys(t), :], qt_ref[plan.side(t), :, cols])
            if t >= first_masked:
                s = jnp.minimum(s, jnp.concatenate([limit_ref[t - first_masked]] * heads, axis=1))
            p_ref[t, :, cols] = s
            plan.fold(tops, t, jnp.max(rows_of_eight(s), axis=0), jnp.maximum, -jnp.inf)
            yield
        for kind in (True, False):
            tops[kind] = jnp.max(tops[kind], axis=0, keepdims=True)

    def exponent(cols, state):
        tops = state["tops"]
        sums = {True: None, False: None}
        for t in range(plan.slots):
            top = plan.pick(t, tops)
            parts = []
            for h in range(heads):
                here = slice(cols.start + h * span, cols.start + (h + 1) * span)
                s = p_ref[t, :, here] - top[:, h * span : (h + 1) * span]
                p = jnp.exp2(s * EXP_SCALE)
                p_ref[t, :, here] = p
                parts.append(jnp.sum(rows_of_eight(p), axis=0))
            plan.fold(sums, t, jnp.concatenate(parts, axis=1), jnp.add, 0.0)
            yield
        for kind, side in ((True, 0), (False, 1)):
            inverse = 1.0 / jnp.sum(sums[kind], axis=0, keepdims=True)
            inv_ref[side : side + 1, cols] = inverse
            gs_ref[side, :, cols] = (gt_ref[side, :, cols].astype(F32) * inverse).astype(BF16)

    def value(cols, state):
        for t in range(plan.slots):
            p = p_ref[t, :, cols].astype(BF16)
            plan.add(acc_ref, t, dot_nt(gs_ref[plan.side(t), :, cols], p))
            yield

    pipeline((score, exponent, value), groups(qt_ref.shape[2], heads))
    plan.unsort(acc_ref, dv_refs, 1.0)


def backward_kernel(n_ctx, span, heads, meta, p_ref, inv_ref, gs_ref, qt_ref, *rest):
    shards = rest[:n_ctx]
    o_ref, ds_ref = rest[n_ctx : n_ctx + 2]
    dk_refs = rest[n_ctx + 2 : 2 * n_ctx + 2]
    v_ref, vt_ref, acc_ref = rest[2 * n_ctx + 2 :]
    plan = Plan(n_ctx, span, meta)
    d = HEAD_DIM
    plan.sort(shards, v_ref)
    for t in range(n_ctx):
        vt_ref[t] = v_ref[t * plan.tile : (t + 1) * plan.tile, :].astype(F32).T.astype(BF16)
    acc_ref[...] = jnp.zeros_like(acc_ref)

    def output(cols, state):
        outs = {True: None, False: None}
        for t in range(plan.slots):
            part = dot_nn(vt_ref[plan.key_tile(t)], p_ref[t, :, cols].astype(BF16))
            plan.fold(outs, t, part, jnp.add, 0.0)
            yield
        state["dots"] = dots = {}
        for kind, side in ((True, 0), (False, 1)):
            out = outs[kind] * inv_ref[side : side + 1, cols]
            for h in range(heads):
                here = slice(cols.start + h * d, cols.start + (h + 1) * d)
                o = out[:, h * span : (h + 1) * span].T.astype(BF16)
                o_ref[pl.ds(plan.row[kind], span), here] = o
            prod = gs_ref[side, :, cols].astype(F32) * out.astype(BF16).astype(F32)
            dots[kind] = jnp.sum(prod, axis=0, keepdims=True)

    def score_grad(cols, state):
        for t in range(plan.slots):
            dp = dot_nn(v_ref[plan.keys(t), :], gs_ref[plan.side(t), :, cols])
            dots = plan.pick(t, state["dots"])
            ds = (p_ref[t, :, cols] * (dp - dots)).astype(BF16)
            ds_ref[t, :, cols] = ds
            plan.add(acc_ref, t, dot_nt(qt_ref[plan.side(t), :, cols], ds))
            yield

    pipeline((output, score_grad), groups(qt_ref.shape[2], heads))
    plan.unsort(acc_ref, dk_refs, SCALE)


def query_kernel(n_ctx, span, heads, meta, ds_ref, k_ref, dq_ref, kt_ref):
    plan = Plan(n_ctx, span, meta)
    d = HEAD_DIM
    for t in range(n_ctx):
        kt_ref[t] = k_ref[t * plan.tile : (t + 1) * plan.tile, :].astype(F32).T.astype(BF16)
    for cols in groups(dq_ref.shape[1], heads):
        dqs = {True: None, False: None}
        for t in range(plan.slots):
            part = dot_nn(kt_ref[plan.key_tile(t)], ds_ref[t, :, cols])
            plan.fold(dqs, t, part, jnp.add, 0.0)
        for kind in (True, False):
            for h in range(heads):
                here = slice(cols.start + h * d, cols.start + (h + 1) * d)
                dq = (dqs[kind][:, h * span : (h + 1) * span] * SCALE).T.astype(BF16)
                dq_ref[pl.ds(plan.row[kind], span), here] = dq


def call(body, out_shape, scratch, flops):
    vmem = pl.BlockSpec(memory_space=pltpu.VMEM)

    def run(meta, *args):
        return pl.pallas_call(
            body,
            in_specs=[vmem] * (1 + len(args)),
            out_specs=[vmem] * len(out_shape),
            out_shape=out_shape,
            scratch_shapes=scratch,
            cost_estimate=pl.CostEstimate(
                flops=flops, bytes_accessed=flops // 512, transcendentals=0
            ),
            compiler_params=pltpu.CompilerParams(vmem_limit_bytes=VMEM_BYTES),
        )(meta, *args)

    return run


def per_device(query_rows, key_rows, value_rows, out_grad, span_order):
    n_ctx = lax.axis_size("ctx")
    n_head = lax.axis_size("head")
    tokens, width = query_rows.shape
    span = tokens // 2
    keys = tokens * n_ctx
    d = HEAD_DIM
    q_heads = width // d
    rows_out = tokens // n_head
    replicas = n_head // KV_HEADS
    heads = math.gcd(q_heads, HEADS)

    def shift(a, r, back=False):
        pairs = [(partner(i, r, n_ctx), i) for i in range(n_ctx)]
        return lax.ppermute(a, "ctx", [p[::-1] for p in pairs] if back else pairs)

    def shape(dims, dtype=BF16):
        return jax.ShapeDtypeStruct(dims, dtype)

    others = range(1, n_ctx)
    order = span_order.reshape(1, 2 * n_ctx)
    kv_group = lax.axis_index("head") * q_heads // GROUP
    own = lax.optimization_barrier(
        jnp.concatenate(
            [lax.dynamic_slice_in_dim(a, kv_group * d, d, 1) for a in (key_rows, value_rows)]
        )
    )
    key_own, value_own = split_own(own)

    def gather(own, name):
        if n_ctx != 4 or name == "value":
            return [own] + [shift(own, r) for r in others]
        near, far = shift(own, 1), shift(own, 2)
        across = lax.ppermute(far, "ctx", [(i ^ 1, i) for i in range(n_ctx)])
        return [own, near, far, across]

    key_shards, value_shards = gather(key_own, "key"), gather(value_own, "value")
    slots = (n_ctx + 1, tokens, q_heads * span)
    rows, pair, shard = shape((tokens, width)), shape((2, q_heads * span), F32), shape((tokens, d))
    work = 2 * slots[0] * slots[1] * slots[2] * d
    bind = lambda f: functools.partial(f, n_ctx, span, heads)
    turned = shape((2, d, q_heads * span))
    total_shape = pltpu.VMEM((2 * n_ctx, d, span), F32)
    queries, grads = call(
        bind(prepare_kernel), [turned, turned], [], work // 10,
    )(order, query_rows, out_grad)
    p, inverse, grads, key_sorted, *value_parts = call(
        bind(forward_kernel),
        [shape(slots, F32), pair, turned, shape((keys, d))] + [shard] * n_ctx,
        [total_shape, pltpu.VMEM((n_ctx + 2 - (n_ctx + 2) // 2, tokens, span), F32)],
        2 * work,
    )(order, queries, grads, *key_shards)
    attn_out, score_grads, *key_parts = call(
        bind(backward_kernel), [rows, shape(slots)] + [shard] * n_ctx,
        [pltpu.VMEM((keys, d), BF16), pltpu.VMEM((n_ctx, d, tokens), BF16), total_shape],
        3 * work,
    )(order, p, inverse, grads, queries, *value_shards)
    (query_grad,) = call(
        bind(query_kernel), [rows],
        [pltpu.VMEM((n_ctx, d, tokens), BF16)], work,
    )(order, score_grads, key_sorted)

    def plus(*parts):
        return functools.reduce(jnp.add, [a.astype(F32) for a in parts])

    if n_ctx == 4:
        far = shift(jnp.concatenate(value_parts[2:]), 2)
        near = plus(value_parts[1], far[tokens:]).astype(BF16)
        near = shift(jnp.concatenate([near, key_parts[1]]), 1)
        value_sum = plus(value_parts[0], far[:tokens], near[:tokens])
        key_sum = plus(key_parts[0], near[tokens:], *[shift(key_parts[r], r) for r in (2, 3)])
    else:
        value_sum, key_sum = [
            plus(parts[0], *[shift(parts[r], r, True) for r in others])
            for parts in (value_parts, key_parts)
        ]
    key_sum, value_sum = key_sum.astype(BF16), value_sum.astype(BF16)
    owned = jnp.concatenate([key_sum, value_sum], axis=1)
    parts = lax.all_to_all(
        owned.reshape(n_head, rows_out, 2 * d), "head", split_axis=0, concat_axis=0
    )
    key_grad, value_grad = total(parts.reshape(KV_HEADS, replicas, rows_out, 2 * d), rows_out)
    return (attn_out, query_grad, key_grad, value_grad)


def total_kernel(x_ref, dk_ref, dv_ref):
    d = HEAD_DIM
    for k in range(x_ref.shape[0]):
        acc = x_ref[k, 0].astype(F32)
        for r in range(1, x_ref.shape[1]):
            acc += x_ref[k, r].astype(F32)
        dk_ref[:, k * d : (k + 1) * d] = acc[:, :d].astype(BF16)
        dv_ref[:, k * d : (k + 1) * d] = acc[:, d:].astype(BF16)


def total(x, rows_out):
    shape = jax.ShapeDtypeStruct((rows_out, KV_HEADS * HEAD_DIM), BF16)
    return pl.pallas_call(
        total_kernel,
        out_shape=[shape, shape],
        compiler_params=pltpu.CompilerParams(vmem_limit_bytes=VMEM_BYTES),
        name="total",
    )(x)


def solution(mesh):
    in_specs = (P("ctx", "head"), P("ctx", None), P("ctx", None), P("ctx", "head"), P())
    out_specs = (
        P("ctx", "head"),
        P("ctx", "head"),
        P(("ctx", "head"), None),
        P(("ctx", "head"), None),
    )

    return jax.shard_map(
        per_device, mesh=mesh, in_specs=in_specs, out_specs=out_specs, check_vma=False
    )
```

```python
import functools
import math

import jax
import jax.numpy as jnp
from jax import lax
from jax.experimental import pallas as pl
from jax.experimental.pallas import tpu as pltpu
from jax.sharding import PartitionSpec as P


KV_HEADS = 8
HEAD_DIM = 128
GROUP = 16
HEADS = 8
VMEM_BYTES = 24 << 20
COVER = 20_000_000_000
F32 = jnp.float32
BF16 = jnp.bfloat16
SCALE = 1.0 / math.sqrt(HEAD_DIM)
EXP_SCALE = SCALE * math.log2(math.e)


def dot_nn(a, b):
    return lax.dot_general(a, b, (((1,), (0,)), ((), ())), preferred_element_type=F32)


def dot_nt(a, b):
    return lax.dot_general(a, b, (((1,), (1,)), ((), ())), preferred_element_type=F32)


def partner(ctx, r, n_ctx):
    return ctx ^ r if n_ctx & (n_ctx - 1) == 0 else (ctx + r) % n_ctx


class Plan:
    def __init__(self, n_ctx, span, meta):
        self.n_ctx, self.span = n_ctx, span
        self.tile = 2 * span
        self.slots = n_ctx + 1
        self.ctx = lax.axis_index("ctx")
        table = meta[...]
        self.order = [table[0, i] for i in range(2 * n_ctx)]
        first, second = self.position(self.ctx, 0), self.position(self.ctx, 1)
        self.hi, self.lo = jnp.maximum(first, second), jnp.minimum(first, second)
        hi_row = pl.multiple_of(jnp.where(first > second, 0, span), span)
        self.row = {True: hi_row, False: pl.multiple_of(span - hi_row, span)}
        self.hi_tiles = (self.hi + 2) // 2
        self.sure_hi = (n_ctx + 2) // 2

    def position(self, ctx, half):
        out = self.order[half]
        for c in range(1, self.n_ctx):
            out = jnp.where(ctx == c, self.order[2 * c + half], out)
        return out

    def kind(self, t):
        if t < self.sure_hi:
            return True
        return False if t == self.slots - 1 else None

    def is_hi(self, t):
        return t < self.hi_tiles

    def key_tile(self, t):
        kind = self.kind(t)
        if kind:
            return t
        if kind is None:
            return jnp.where(self.is_hi(t), t, t - self.hi_tiles)
        return t - self.hi_tiles

    def keys(self, t):
        return pl.ds(pl.multiple_of(self.key_tile(t) * self.tile, self.tile), self.tile)

    def pick(self, t, pair):
        kind = self.kind(t)
        if kind is None:
            return jnp.where(self.is_hi(t), pair[True], pair[False])
        return pair[kind]

    def fold(self, acc, t, part, op, neutral):
        for kind in (True, False):
            if self.kind(t) is None:
                use = self.is_hi(t) if kind else jnp.logical_not(self.is_hi(t))
                term = jnp.where(use, part, neutral)
            elif self.kind(t) == kind:
                term = part
            else:
                continue
            acc[kind] = term if acc[kind] is None else op(acc[kind], term)

    def sort(self, shards, out):
        for r, shard in enumerate(shards):
            src = partner(self.ctx, r, self.n_ctx)
            for half in range(2):
                pos = self.position(src, half)
                rows = pl.ds(pl.multiple_of(pos * self.span, self.span), self.span)
                out[rows, :] = shard[half * self.span : (half + 1) * self.span, :]

    def unsort(self, acc, outs, scale):
        for r, out in enumerate(outs):
            dest = partner(self.ctx, r, self.n_ctx)
            for half in range(2):
                block = acc[self.position(dest, half)] * scale
                out[half * self.span : (half + 1) * self.span, :] = block.T.astype(BF16)

    def side(self, t):
        return self.pick(t, {True: 0, False: 1})

    def add(self, acc, t, part):
        block = 2 * self.key_tile(t)
        acc[block] += part[:, : self.span]
        acc[block + 1] += part[:, self.span :]


def pipeline(stages, parts):
    states = [{} for _ in parts]
    for step in range(len(parts) + len(stages) - 1):
        running = [
            stage(parts[step - k], states[step - k])
            for k, stage in reversed(list(enumerate(stages)))
            if 0 <= step - k < len(parts)
        ]
        while running:
            running = [r for r in running if next(r, running) is not running]


def groups(width, heads):
    step = heads * HEAD_DIM
    return [slice(c, c + step) for c in range(0, width, step)]


def own_kernel(kv_ref, k_ref, v_ref):
    tokens = k_ref.shape[0]
    k_ref[...] = kv_ref[:tokens, :]
    v_ref[...] = kv_ref[tokens:, :]


def split_own(own):
    vmem = pl.BlockSpec(memory_space=pltpu.VMEM)
    shape = jax.ShapeDtypeStruct((own.shape[0] // 2, own.shape[1]), BF16)
    return pl.pallas_call(
        own_kernel,
        in_specs=[vmem],
        out_specs=[vmem, vmem],
        out_shape=[shape, shape],
        cost_estimate=pl.CostEstimate(flops=COVER, bytes_accessed=0, transcendentals=0),
        compiler_params=pltpu.CompilerParams(vmem_limit_bytes=VMEM_BYTES),
        name="own",
    )(own)


def prepare_kernel(n_ctx, span, heads, meta, q_ref, g_ref, qt_ref, gt_ref):
    plan = Plan(n_ctx, span, meta)
    d = HEAD_DIM
    for src, dst in ((q_ref, qt_ref), (g_ref, gt_ref)):
        for kind, side in ((True, 0), (False, 1)):
            for h in range(src.shape[1] // d):
                block = src[pl.ds(plan.row[kind], span), h * d : (h + 1) * d]
                dst[side, :, h * span : (h + 1) * span] = block.astype(F32).T.astype(BF16)


def forward_kernel(n_ctx, span, heads, meta, qt_ref, gt_ref, *rest):
    shards = rest[:n_ctx]
    p_ref, inv_ref, gs_ref, k_ref = rest[n_ctx : n_ctx + 4]
    dv_refs = rest[n_ctx + 4 : 2 * n_ctx + 4]
    acc_ref, limit_ref = rest[2 * n_ctx + 4 :]
    plan = Plan(n_ctx, span, meta)
    plan.sort(shards, k_ref)
    acc_ref[...] = jnp.zeros_like(acc_ref)
    first_masked = plan.sure_hi - 1
    dims = (plan.tile, span)
    diff = lax.broadcasted_iota(jnp.int32, dims, 0) - lax.broadcasted_iota(jnp.int32, dims, 1)
    for t in range(first_masked, plan.slots):
        position = plan.pick(t, {True: plan.hi, False: plan.lo})
        seen = diff <= position * span - plan.key_tile(t) * plan.tile
        limit_ref[t - first_masked] = jnp.where(seen, jnp.inf, -jnp.inf)

    def rows_of_eight(x):
        return x.reshape(x.shape[0] // 8, 8, x.shape[1])

    def score(cols, state):
        state["tops"] = tops = {True: None, False: None}
        for t in range(plan.slots):
            s = dot_nn(k_ref[plan.keys(t), :], qt_ref[plan.side(t), :, cols])
            if t >= first_masked:
                s = jnp.minimum(s, jnp.concatenate([limit_ref[t - first_masked]] * heads, axis=1))
            p_ref[t, :, cols] = s
            plan.fold(tops, t, jnp.max(rows_of_eight(s), axis=0), jnp.maximum, -jnp.inf)
            yield
        for kind in (True, False):
            tops[kind] = jnp.max(tops[kind], axis=0, keepdims=True)

    def exponent(cols, state):
        tops = state["tops"]
        sums = {True: None, False: None}
        for t in range(plan.slots):
            top = plan.pick(t, tops)
            parts = []
            for h in range(heads):
                here = slice(cols.start + h * span, cols.start + (h + 1) * span)
                s = p_ref[t, :, here] - top[:, h * span : (h + 1) * span]
                p = jnp.exp2(s * EXP_SCALE)
                p_ref[t, :, here] = p
                parts.append(jnp.sum(rows_of_eight(p), axis=0))
            plan.fold(sums, t, jnp.concatenate(parts, axis=1), jnp.add, 0.0)
            yield
        for kind, side in ((True, 0), (False, 1)):
            inverse = 1.0 / jnp.sum(sums[kind], axis=0, keepdims=True)
            inv_ref[side : side + 1, cols] = inverse
            gs_ref[side, :, cols] = (gt_ref[side, :, cols].astype(F32) * inverse).astype(BF16)

    def value(cols, state):
        for t in range(plan.slots):
            p = p_ref[t, :, cols].astype(BF16)
            plan.add(acc_ref, t, dot_nt(gs_ref[plan.side(t), :, cols], p))
            yield

    pipeline((score, exponent, value), groups(qt_ref.shape[2], heads))
    plan.unsort(acc_ref, dv_refs, 1.0)


def backward_kernel(n_ctx, span, heads, meta, p_ref, inv_ref, gs_ref, qt_ref, *rest):
    shards = rest[:n_ctx]
    o_ref, ds_ref = rest[n_ctx : n_ctx + 2]
    dk_refs = rest[n_ctx + 2 : 2 * n_ctx + 2]
    v_ref, vt_ref, acc_ref = rest[2 * n_ctx + 2 :]
    plan = Plan(n_ctx, span, meta)
    d = HEAD_DIM
    plan.sort(shards, v_ref)
    for t in range(n_ctx):
        vt_ref[t] = v_ref[t * plan.tile : (t + 1) * plan.tile, :].astype(F32).T.astype(BF16)
    acc_ref[...] = jnp.zeros_like(acc_ref)

    def output(cols, state):
        outs = {True: None, False: None}
        for t in range(plan.slots):
            part = dot_nn(vt_ref[plan.key_tile(t)], p_ref[t, :, cols].astype(BF16))
            plan.fold(outs, t, part, jnp.add, 0.0)
            yield
        state["dots"] = dots = {}
        for kind, side in ((True, 0), (False, 1)):
            out = outs[kind] * inv_ref[side : side + 1, cols]
            for h in range(heads):
                here = slice(cols.start + h * d, cols.start + (h + 1) * d)
                o = out[:, h * span : (h + 1) * span].T.astype(BF16)
                o_ref[pl.ds(plan.row[kind], span), here] = o
            prod = gs_ref[side, :, cols].astype(F32) * out.astype(BF16).astype(F32)
            dots[kind] = jnp.sum(prod, axis=0, keepdims=True)

    def score_grad(cols, state):
        for t in range(plan.slots):
            dp = dot_nn(v_ref[plan.keys(t), :], gs_ref[plan.side(t), :, cols])
            dots = plan.pick(t, state["dots"])
            ds = (p_ref[t, :, cols] * (dp - dots)).astype(BF16)
            ds_ref[t, :, cols] = ds
            plan.add(acc_ref, t, dot_nt(qt_ref[plan.side(t), :, cols], ds))
            yield

    pipeline((output, score_grad), groups(qt_ref.shape[2], heads))
    plan.unsort(acc_ref, dk_refs, SCALE)


def query_kernel(n_ctx, span, heads, meta, ds_ref, k_ref, dq_ref, kt_ref):
    plan = Plan(n_ctx, span, meta)
    d = HEAD_DIM
    for t in range(n_ctx):
        kt_ref[t] = k_ref[t * plan.tile : (t + 1) * plan.tile, :].astype(F32).T.astype(BF16)
    for cols in groups(dq_ref.shape[1], heads):
        dqs = {True: None, False: None}
        for t in range(plan.slots):
            part = dot_nn(kt_ref[plan.key_tile(t)], ds_ref[t, :, cols])
            plan.fold(dqs, t, part, jnp.add, 0.0)
        for kind in (True, False):
            for h in range(heads):
                here = slice(cols.start + h * d, cols.start + (h + 1) * d)
                dq = (dqs[kind][:, h * span : (h + 1) * span] * SCALE).T.astype(BF16)
                dq_ref[pl.ds(plan.row[kind], span), here] = dq


def call(body, out_shape, scratch, flops):
    vmem = pl.BlockSpec(memory_space=pltpu.VMEM)

    def run(meta, *args):
        return pl.pallas_call(
            body,
            in_specs=[vmem] * (1 + len(args)),
            out_specs=[vmem] * len(out_shape),
            out_shape=out_shape,
            scratch_shapes=scratch,
            cost_estimate=pl.CostEstimate(
                flops=flops, bytes_accessed=flops // 512, transcendentals=0
            ),
            compiler_params=pltpu.CompilerParams(vmem_limit_bytes=VMEM_BYTES),
        )(meta, *args)

    return run


def per_device(query_rows, key_rows, value_rows, out_grad, span_order):
    n_ctx = lax.axis_size("ctx")
    n_head = lax.axis_size("head")
    tokens, width = query_rows.shape
    span = tokens // 2
    keys = tokens * n_ctx
    d = HEAD_DIM
    q_heads = width // d
    rows_out = tokens // n_head
    replicas = n_head // KV_HEADS
    heads = math.gcd(q_heads, HEADS)

    def shift(a, r, back=False):
        pairs = [(partner(i, r, n_ctx), i) for i in range(n_ctx)]
        return lax.ppermute(a, "ctx", [p[::-1] for p in pairs] if back else pairs)

    def shape(dims, dtype=BF16):
        return jax.ShapeDtypeStruct(dims, dtype)

    others = range(1, n_ctx)
    order = span_order.reshape(1, 2 * n_ctx)
    kv_group = lax.axis_index("head") * q_heads // GROUP
    own = lax.optimization_barrier(
        jnp.concatenate(
            [lax.dynamic_slice_in_dim(a, kv_group * d, d, 1) for a in (key_rows, value_rows)]
        )
    )
    key_own, value_own = split_own(own)

    def gather(own, name):
        if n_ctx != 4 or name == "value":
            return [own] + [shift(own, r) for r in others]
        near, far = shift(own, 1), shift(own, 2)
        across = lax.ppermute(far, "ctx", [(i ^ 1, i) for i in range(n_ctx)])
        return [own, near, far, across]

    key_shards, value_shards = gather(key_own, "key"), gather(value_own, "value")
    slots = (n_ctx + 1, tokens, q_heads * span)
    rows, pair, shard = shape((tokens, width)), shape((2, q_heads * span), F32), shape((tokens, d))
    work = 2 * slots[0] * slots[1] * slots[2] * d
    bind = lambda f: functools.partial(f, n_ctx, span, heads)
    turned = shape((2, d, q_heads * span))
    total_shape = pltpu.VMEM((2 * n_ctx, d, span), F32)
    queries, grads = call(
        bind(prepare_kernel), [turned, turned], [], work // 10,
    )(order, query_rows, out_grad)
    p, inverse, grads, key_sorted, *value_parts = call(
        bind(forward_kernel),
        [shape(slots, F32), pair, turned, shape((keys, d))] + [shard] * n_ctx,
        [total_shape, pltpu.VMEM((n_ctx + 2 - (n_ctx + 2) // 2, tokens, span), F32)],
        2 * work,
    )(order, queries, grads, *key_shards)
    attn_out, score_grads, *key_parts = call(
        bind(backward_kernel), [rows, shape(slots)] + [shard] * n_ctx,
        [pltpu.VMEM((keys, d), BF16), pltpu.VMEM((n_ctx, d, tokens), BF16), total_shape],
        3 * work,
    )(order, p, inverse, grads, queries, *value_shards)
    (query_grad,) = call(
        bind(query_kernel), [rows],
        [pltpu.VMEM((n_ctx, d, tokens), BF16)], work,
    )(order, score_grads, key_sorted)

    def plus(*parts):
        return functools.reduce(jnp.add, [a.astype(F32) for a in parts])

    if n_ctx == 4:
        near = shift(jnp.concatenate([value_parts[1], value_parts[3]]), 1)
        far = plus(value_parts[2], near[tokens:]).astype(BF16)
        far = shift(jnp.concatenate([far, key_parts[2]]), 2)
        value_sum = plus(value_parts[0], near[:tokens], far[:tokens])
        key_sum = plus(key_parts[0], far[tokens:], *[shift(key_parts[r], r) for r in (1, 3)])
    else:
        value_sum, key_sum = [
            plus(parts[0], *[shift(parts[r], r, True) for r in others])
            for parts in (value_parts, key_parts)
        ]
    key_sum, value_sum = key_sum.astype(BF16), value_sum.astype(BF16)
    owned = jnp.concatenate([key_sum, value_sum], axis=1)
    parts = lax.all_to_all(
        owned.reshape(n_head, rows_out, 2 * d), "head", split_axis=0, concat_axis=0
    )
    key_grad, value_grad = total(parts.reshape(KV_HEADS, replicas, rows_out, 2 * d), rows_out)
    return (attn_out, query_grad, key_grad, value_grad)


def total_kernel(x_ref, dk_ref, dv_ref):
    d = HEAD_DIM
    for k in range(x_ref.shape[0]):
        acc = x_ref[k, 0].astype(F32)
        for r in range(1, x_ref.shape[1]):
            acc += x_ref[k, r].astype(F32)
        dk_ref[:, k * d : (k + 1) * d] = acc[:, :d].astype(BF16)
        dv_ref[:, k * d : (k + 1) * d] = acc[:, d:].astype(BF16)


def total(x, rows_out):
    shape = jax.ShapeDtypeStruct((rows_out, KV_HEADS * HEAD_DIM), BF16)
    return pl.pallas_call(
        total_kernel,
        out_shape=[shape, shape],
        compiler_params=pltpu.CompilerParams(vmem_limit_bytes=VMEM_BYTES),
        name="total",
    )(x)


def solution(mesh):
    in_specs = (P("ctx", "head"), P("ctx", None), P("ctx", None), P("ctx", "head"), P())
    out_specs = (
        P("ctx", "head"),
        P("ctx", "head"),
        P(("ctx", "head"), None),
        P(("ctx", "head"), None),
    )

    return jax.shard_map(
        per_device, mesh=mesh, in_specs=in_specs, out_specs=out_specs, check_vma=False
    )
```
